32 devices in a mesh: tile: 8 (over z, y), member: 4 (over x, core).
Axes of the slice: x: 2, y: 2, z: 4, core: 2. Of those that a mesh axis runs over, the one named last changes fastest.
Arguments:
- states: bfloat16 [4, 2048, 512], P('member', 'tile'), may hold values from -105 to 105
- teacher: bfloat16 [2048, 512], P('tile'), may hold values from -6 to 6
- w_qkv: bfloat16 [512, 1536], replicated, may hold values from -0.25 to 0.25
- w_out: bfloat16 [512, 512], replicated, may hold values from -0.25 to 0.25
- gain: float32 [512], replicated, may hold values from 0.1 to 1.9
- bias: float32 [8, 64, 64], replicated, may hold values from -4 to 400
- neighbours: int32 [32, 9], P('tile'), may hold values from 0 to 31, as said below
- valid: int32 [32, 9], P('tile'), may hold values from 0 to 1, as said below
- orient: int32 [32, 9], P('tile'), may hold values from 0 to 3, as said below
Outputs:
- output: bfloat16 [4, 2048, 512], P('member', 'tile')
- d_states: bfloat16 [4, 2048, 512], P('member', 'tile')
- d_wqkv: float32 [512, 1536], P('tile', 'member')
- d_wout: float32 [512, 512], P('tile', 'member')
- d_gain: float32 [512], replicated
- d_bias: float32 [8, 64, 64], replicated
The draws below stay inside these ranges and needn't reach their ends.
Inputs may be any that keep to these rules, and one draw needn't show every extreme that they name: `neighbours`: for a block in column c, slots 3 m, 3 m + 1 and 3 m + 2 name blocks of column c + m - 1, block = column * 4 + row; where c + m - 1 lies outside 0 to 8 - 1 (the window's open ends) these slots name the block itself; slot 4 names the block itself. `valid`: slot 4 is always 1; slots whose column lies outside the window are 0. `orient`: slot 4 is always 0.
All inputs are finite; a program needn't handle non-finite values.
Results may differ from the reference program's by a relative error of at most 0.008.
Values may be sent and summed in bfloat16 or wider, within the bound.
No kernel may reach another device: no remote copies, remote signals or barrier semaphores. Data moves between devices by JAX's collectives and lax.ppermute only.
A program may use at most 128 MiB of HBM per device.

```python
import jax
import jax.numpy as jnp
from jax import lax

D = 512
HEADS = 8
HD = 64
SIDE = 8
PIX = 64
ROWS = 4
SLOTS = 9
COLS = 8
BLOCKS = 32
PIXELS = 2048
MEMBERS = 4


def draw_states(key, part):
    keys = jax.random.split(key, 3)
    base = jnp.clip(jax.random.normal(keys[0], (MEMBERS, PIXELS, D), jnp.float32), -6.0, 6.0)
    row_scale = jnp.exp(jax.random.uniform(keys[1], (MEMBERS, PIXELS, 1), jnp.float32, -1.15, 1.15))
    column_scale = jnp.exp(jax.random.uniform(keys[2], (1, 1, D), jnp.float32, -1.15, 1.15))
    rising = jnp.exp(jnp.log(3.0) * (jnp.arange(PIXELS, dtype=jnp.float32) / PIXELS - 0.5))[None, :, None]
    return (base * row_scale * column_scale * rising).astype(jnp.bfloat16)


def draw_bias(key, part):
    base = jnp.clip(jax.random.normal(key, (HEADS, PIX, PIX), jnp.float32), -4.0, 4.0)
    return base


def outside_window():
    blocks = jnp.arange(BLOCKS, dtype=jnp.int32)[:, None]
    slots = jnp.arange(SLOTS, dtype=jnp.int32)[None, :]
    column = blocks // ROWS + slots // 3 - 1
    return (column < 0) | (column >= COLS)


def draw_neighbours(key, part):
    blocks = jnp.arange(BLOCKS, dtype=jnp.int32)[:, None]
    slots = jnp.arange(SLOTS, dtype=jnp.int32)[None, :]
    row_pick = jax.random.randint(key, (BLOCKS, SLOTS), 0, ROWS, dtype=jnp.int32)
    column = blocks // ROWS + slots // 3 - 1
    named = column * ROWS + row_pick
    return jnp.where((slots == 4) | outside_window(), blocks, named).astype(jnp.int32)


def draw_valid(key, part):
    slots = jnp.arange(SLOTS, dtype=jnp.int32)[None, :]
    pick = jax.random.randint(jax.random.fold_in(key, 11), (BLOCKS, SLOTS), 0, 4, dtype=jnp.int32)
    kept = jnp.where(outside_window(), 0, jnp.where(pick > 0, 1, 0))
    return jnp.where(slots == 4, 1, kept).astype(jnp.int32)


def draw_orient(key, part):
    slots = jnp.arange(SLOTS, dtype=jnp.int32)[None, :]
    pick = jax.random.randint(jax.random.fold_in(key, 23), (BLOCKS, SLOTS), 0, 4, dtype=jnp.int32)
    return jnp.where(slots == 4, 0, pick).astype(jnp.int32)


def levels(stream_key, shape, pieces, low, largest):
    level = 1.0
    for dim, shards_of in pieces:
        draws = jax.random.uniform(jax.random.fold_in(jax.random.fold_in(stream_key, 6), dim), (shards_of,), jnp.float32, low / len(pieces), largest / len(pieces))
        level = level * jnp.repeat(jnp.exp(draws), shape[dim] // shards_of).reshape((-1,) + (1,) * (len(shape) - 1 - dim))
    return level


def scatter_about(key, dims, spread, limit, cuts=(), kind=jnp.bfloat16):
    array = spread * jax.random.normal(key, dims, jnp.float32)
    if cuts:
        array = array * levels(key, dims, cuts, -0.22, 0.18)
    return jnp.clip(array, -limit, limit).astype(kind)


def setup_inputs(seed: int = 0) -> dict:
    key_list = jax.random.split(jax.random.key(seed), 10)
    states = draw_states(jax.random.fold_in(key_list[9], 71), 0)
    teacher = scatter_about(key_list[1], (PIXELS, D), 1.0, 6.0, ((0, 8),))
    w_qkv = scatter_about(key_list[2], (D, 3 * D), D ** -0.5, 0.25)
    w_out = scatter_about(key_list[3], (D, D), D ** -0.5, 0.25)
    gain = jnp.clip(1.0 + 0.18 * jax.random.normal(key_list[4], (D,), jnp.float32), 0.1, 1.9)
    bias = draw_bias(jax.random.fold_in(key_list[9], 71), 0)
    neighbours = draw_neighbours(jax.random.fold_in(key_list[9], 71), 0)
    valid = draw_valid(jax.random.fold_in(key_list[9], 71), 0)
    orient = draw_orient(jax.random.fold_in(key_list[9], 71), 0)
    return {"states": states, "teacher": teacher, "w_qkv": w_qkv, "w_out": w_out, "gain": gain, "bias": bias, "neighbours": neighbours, "valid": valid, "orient": orient}


EPS = 1e-06
NEG = -1e+30
HIGH = lax.Precision.HIGHEST

def turn_onehot():
    position = jnp.arange(PIX, dtype=jnp.int32)
    upper = position // SIDE
    lower = position % SIDE
    tables = []
    for turn in range(4):
        tables.append(upper * SIDE + lower)
        upper, lower = (lower, SIDE - 1 - upper)
    table = jnp.stack(tables)
    return (table[:, :, None] == position[None, None, :]).astype(jnp.float32)

def probabilities(queries, keys_near, alive, turn_pick, turned):
    scores = jnp.einsum('gihd,gsjhd->ghisj', queries.astype(jnp.float32), keys_near.astype(jnp.float32)) * HD ** (-0.5)
    scores = scores + jnp.einsum('gsk,khij->ghisj', turn_pick, turned, precision=HIGH)
    inside = alive[:, None, None, :, None]
    masked = jnp.where(inside, scores, NEG)
    highest = lax.optimization_barrier(jnp.max(masked, axis=(3, 4), keepdims=True))
    weights = jnp.where(inside, jnp.exp(masked - highest), 0.0)
    return weights / lax.optimization_barrier(jnp.sum(weights, axis=(3, 4), keepdims=True))

def member_pass(inputs, teacher, w_qkv, w_out, gain, turned, near_cols, alive_cols, pick_cols):
    inputs32 = inputs.astype(jnp.float32)
    inverse = lax.rsqrt(lax.optimization_barrier(jnp.mean(inputs32 * inputs32, axis=-1, keepdims=True)) + EPS)
    normed = (inputs32 * inverse * gain).astype(jnp.bfloat16)
    projected = jnp.dot(normed, w_qkv, preferred_element_type=jnp.float32).astype(jnp.bfloat16)
    queries = projected[:, :D].reshape(COLS, ROWS, PIX, HEADS, HD)
    keys_all = projected[:, D:2 * D].reshape(BLOCKS, PIX, HEADS, HD)
    values_all = projected[:, 2 * D:].reshape(BLOCKS, PIX, HEADS, HD)

    def forward_column(packed):
        query_col, near_col, alive_col, pick_col = packed
        keys_near = keys_all[near_col]
        values_near = values_all[near_col]
        probs = probabilities(query_col, keys_near, alive_col, pick_col, turned)
        probs_low = probs.astype(jnp.bfloat16)
        return jnp.einsum('ghisj,gsjhd->gihd', probs_low.astype(jnp.float32), values_near.astype(jnp.float32)).astype(jnp.bfloat16)
    mixed = lax.map(forward_column, (queries, near_cols, alive_cols, pick_cols)).reshape(PIXELS, D)
    output32 = inputs32 + jnp.dot(mixed, w_out, preferred_element_type=jnp.float32)
    d_output = (output32 - teacher.astype(jnp.float32)).astype(jnp.bfloat16)
    d_mixed = jnp.dot(d_output, w_out.T, preferred_element_type=jnp.float32).astype(jnp.bfloat16)
    d_mixed = d_mixed.reshape(COLS, ROWS, PIX, HEADS, HD)

    def backward_column(carry, packed):
        d_keyval, d_turned = carry
        query_col, dmix_col, near_col, alive_col, pick_col = packed
        keys_near = keys_all[near_col]
        values_near = values_all[near_col]
        probs = probabilities(query_col, keys_near, alive_col, pick_col, turned)
        probs_low = probs.astype(jnp.bfloat16)
        d_probs = jnp.einsum('gihd,gsjhd->ghisj', dmix_col.astype(jnp.float32), values_near.astype(jnp.float32))
        delta_sum = lax.optimization_barrier(jnp.sum(probs * d_probs, axis=(3, 4), keepdims=True))
        d_scores = probs * (d_probs - delta_sum)
        d_scores_low = d_scores.astype(jnp.bfloat16).astype(jnp.float32)
        d_queries = (jnp.einsum('ghisj,gsjhd->gihd', d_scores_low, keys_near.astype(jnp.float32)) * HD ** (-0.5)).astype(jnp.bfloat16)
        d_keys = jnp.einsum('ghisj,gihd->gsjhd', d_scores_low, query_col.astype(jnp.float32)) * HD ** (-0.5)
        d_values = jnp.einsum('ghisj,gihd->gsjhd', probs_low.astype(jnp.float32), dmix_col.astype(jnp.float32))
        both = jnp.concatenate([d_keys.reshape(ROWS * SLOTS, PIX, D), d_values.reshape(ROWS * SLOTS, PIX, D)], axis=-1)
        d_keyval = d_keyval.at[near_col.reshape(-1)].add(both)
        d_turned = d_turned + jnp.einsum('gsk,ghisj->khij', pick_col, d_scores, precision=HIGH)
        return ((d_keyval, d_turned), d_queries)
    start_carry = (jnp.zeros((BLOCKS, PIX, 2 * D), jnp.float32), jnp.zeros((4, HEADS, PIX, PIX), jnp.float32))
    (d_keyval, d_turned), d_queries = lax.scan(backward_column, start_carry, (queries, d_mixed, near_cols, alive_cols, pick_cols))
    d_proj = jnp.concatenate([d_queries.reshape(PIXELS, D), d_keyval.reshape(PIXELS, 2 * D).astype(jnp.bfloat16)], axis=-1)
    d_normed = jnp.dot(d_proj, w_qkv.T, preferred_element_type=jnp.float32)
    d_gain = lax.optimization_barrier(jnp.sum(d_normed * inputs32 * inverse, axis=0))
    d_scaled = d_normed * gain
    d_inputs = d_output.astype(jnp.float32) + inverse * d_scaled - inputs32 * inverse * inverse * inverse * lax.optimization_barrier(jnp.mean(d_scaled * inputs32, axis=-1, keepdims=True))
    d_wqkv = jnp.dot(normed.T, d_proj, preferred_element_type=jnp.float32)
    d_wout = jnp.dot(mixed.T, d_output, preferred_element_type=jnp.float32)
    return (output32.astype(jnp.bfloat16), d_inputs.astype(jnp.bfloat16), d_wqkv, d_wout, d_gain, d_turned)

def reference(states, teacher, w_qkv, w_out, gain, bias, neighbours, valid, orient):
    onehot_turn = turn_onehot()
    turned = jnp.einsum('ail,kjl->kaij', bias, onehot_turn, precision=HIGH)
    near_cols = neighbours.reshape(COLS, ROWS, SLOTS)
    alive_cols = (valid > 0).reshape(COLS, ROWS, SLOTS)
    pick_cols = (orient[:, :, None] == jnp.arange(4, dtype=jnp.int32)[None, None, :]).astype(jnp.float32).reshape(COLS, ROWS, SLOTS, 4)

    def one_member(inputs):
        return member_pass(inputs, teacher, w_qkv, w_out, gain, turned, near_cols, alive_cols, pick_cols)
    output, d_states, d_wqkv, d_wout, d_gain, d_turned = lax.map(one_member, states)
    d_bias = jnp.einsum('khij,kjl->hil', lax.optimization_barrier(jnp.sum(d_turned, axis=0)), onehot_turn, precision=HIGH)
    return (output, d_states, lax.optimization_barrier(jnp.sum(d_wqkv, axis=0)), lax.optimization_barrier(jnp.sum(d_wout, axis=0)), lax.optimization_barrier(jnp.sum(d_gain, axis=0)), d_bias)
```

```python
import functools

import jax
import jax.numpy as jnp
from jax import lax
from jax.experimental import pallas as pl
from jax.experimental.pallas import tpu as pltpu
from jax.sharding import PartitionSpec as P

HD = 64
SIDE = 8
PIX = 64
ROWS = 4
SLOTS = 9
PAD_SLOTS = 10
PAIRS = PAD_SLOTS // 2
GROUP = 4
TURNS = 4
COL_DEV = 1

EPS = 1e-06
NEG = -1e30
HIGH = lax.Precision.HIGHEST
BF = jnp.bfloat16
F32 = jnp.float32

VM = pltpu.MemorySpace.VMEM
SM = pltpu.MemorySpace.SMEM


def nn(a, b):
    return jnp.dot(a, b, preferred_element_type=F32)


def nt(a, b):
    return lax.dot_general(a, b, (((1,), (1,)), ((), ())), preferred_element_type=F32)


def tn(a, b):
    return lax.dot_general(a, b, (((0,), (0,)), ((), ())), preferred_element_type=F32)


def turn_index(position, turn):
    upper = position // SIDE
    lower = position % SIDE
    for _ in range(turn):
        upper, lower = lower, SIDE - 1 - upper
    return upper * SIDE + lower


def rms(x32):
    return lax.rsqrt(jnp.mean(x32 * x32, axis=-1, keepdims=True) + EPS)


def own_kernel(x_ref, gain_ref, w_ref, bias_ref, normed_ref, proj_ref, table_ref):
    x32 = x_ref[...].astype(F32)
    normed = (x32 * rms(x32) * gain_ref[...]).astype(BF)
    normed_ref[...] = normed
    proj_ref[...] = nn(normed, w_ref[...]).astype(BF)
    source = lax.broadcasted_iota(jnp.int32, (PIX, 2 * PIX), 0)
    target = lax.broadcasted_iota(jnp.int32, (PIX, 2 * PIX), 1) & (PIX - 1)
    for turn in range(TURNS):
        pick = (turn_index(target, turn) == source).astype(F32)
        table_ref[turn] = jnp.dot(bias_ref[...], pick, preferred_element_type=F32, precision=HIGH)


def attention_kernel(
    near_ref, turn_ref, drop_ref,
    x_ref, xl_ref, xr_ref, proj_ref, table_ref, gain_ref, w_ref, wo_ref, teacher_ref,
    out_ref, dout_ref, mixed_ref, dq_ref, own_ref, left_ref, right_ref, bias_ref,
    kv, cat, prob, dmix, acc, tacc,
):
    dim = x_ref.shape[1]
    rows = x_ref.shape[0]
    blocks = rows // PIX
    groups = dim // (GROUP * HD)
    wide = GROUP * HD
    scale = HD ** -0.5
    head_of = lax.broadcasted_iota(jnp.int32, (PIX, wide), 1) // HD
    low_half = lax.broadcasted_iota(jnp.int32, (wide, 2 * PIX), 1) < PIX
    low_row = lax.broadcasted_iota(jnp.int32, (1, 2 * PIX), 1) < PIX

    def stacked(block):
        return jnp.concatenate(
            [jnp.where(head_of == h, block, 0.0) for h in range(GROUP)], axis=0
        ).astype(BF)

    def unstacked(tall):
        picked = tall[:PIX]
        for h in range(1, GROUP):
            picked = jnp.where(head_of == h, tall[h * PIX : (h + 1) * PIX], picked)
        return picked

    kv[rows : 2 * rows, :] = proj_ref[:, dim:]
    for side_ref, at in ((xl_ref, 0), (xr_ref, 2 * rows)):
        s32 = side_ref[...].astype(F32)
        normed = (s32 * rms(s32) * gain_ref[...]).astype(BF)
        kv[at : at + rows, :] = nn(normed, w_ref[:, dim:]).astype(BF)
    acc[...] = jnp.zeros_like(acc)
    tacc[...] = jnp.zeros_like(tacc)

    def forward(b, carry):
        for s in range(PAD_SLOTS):
            start = pl.multiple_of(near_ref[b * PAD_SLOTS + s] * PIX, PIX)
            cat[b, s * PIX : (s + 1) * PIX, :] = kv[pl.ds(start, PIX), :]
        base = pl.multiple_of(b * PIX, PIX)
        for g in range(groups):
            lanes = slice(g * wide, (g + 1) * wide)
            q = stacked(proj_ref[pl.ds(base, PIX), lanes].astype(F32) * scale)
            scores = nt(q, cat[b, :, lanes])
            parts = []
            for p in range(PAIRS):
                first = b * PAD_SLOTS + 2 * p
                low = table_ref[turn_ref[first], lanes, :]
                high = table_ref[turn_ref[first + 1], lanes, :]
                drop = jnp.where(low_row, drop_ref[first], drop_ref[first + 1])
                tile = scores[:, p * 2 * PIX : (p + 1) * 2 * PIX]
                parts.append(tile + jnp.where(low_half, low, high) + drop)
            full = jnp.concatenate(parts, axis=1)
            highest = jnp.max(full, axis=1, keepdims=True)
            weights = jnp.exp(full - highest)
            probs = weights * (1.0 / jnp.sum(weights, axis=1, keepdims=True))
            prob[b, lanes, :] = probs
            tall = nn(probs.astype(BF), cat[b, :, dim + g * wide : dim + (g + 1) * wide])
            mixed_ref[pl.ds(base, PIX), lanes] = unstacked(tall).astype(BF)
        return carry

    lax.fori_loop(0, blocks, forward, 0)

    out32 = x_ref[...].astype(F32) + nn(mixed_ref[...], wo_ref[...])
    out_ref[...] = out32.astype(BF)
    d_out = (out32 - teacher_ref[...].astype(F32)).astype(BF)
    dout_ref[...] = d_out
    dmix[...] = nt(d_out, wo_ref[...]).astype(BF)

    def backward(b, carry):
        base = pl.multiple_of(b * PIX, PIX)
        for g in range(groups):
            lanes = slice(g * wide, (g + 1) * wide)
            upper = slice(dim + g * wide, dim + (g + 1) * wide)
            q = stacked(proj_ref[pl.ds(base, PIX), lanes].astype(F32) * scale)
            dm = stacked(dmix[pl.ds(base, PIX), lanes].astype(F32))
            probs = prob[b, lanes, :]
            d_probs = nt(dm, cat[b, :, upper])
            delta = jnp.sum(probs * d_probs, axis=1, keepdims=True)
            d_scores = probs * (d_probs - delta)
            d_low = d_scores.astype(BF)
            tall = nn(d_low, cat[b, :, lanes])
            dq_ref[pl.ds(base, PIX), lanes] = (unstacked(tall) * scale).astype(BF)
            d_k = tn(d_low, q)
            d_v = tn(probs.astype(BF), dm)
            for s in range(SLOTS):
                start = pl.multiple_of(near_ref[b * PAD_SLOTS + s] * PIX, PIX)
                acc[pl.ds(start, PIX), lanes] += d_k[s * PIX : (s + 1) * PIX]
                acc[pl.ds(start, PIX), upper] += d_v[s * PIX : (s + 1) * PIX]
            for p in range(PAIRS):
                first = b * PAD_SLOTS + 2 * p
                tile = d_scores[:, p * 2 * PIX : (p + 1) * 2 * PIX]
                tacc[turn_ref[first], lanes, :] += jnp.where(low_half, tile, 0.0)
                tacc[turn_ref[first + 1], lanes, :] += jnp.where(low_half, 0.0, tile)
        return carry

    lax.fori_loop(0, blocks, backward, 0)

    left_ref[...] = acc[:rows, :].astype(BF)
    own_ref[...] = acc[rows : 2 * rows, :]
    right_ref[...] = acc[2 * rows :, :].astype(BF)
    source = lax.broadcasted_iota(jnp.int32, (2 * PIX, PIX), 0) & (PIX - 1)
    target = lax.broadcasted_iota(jnp.int32, (2 * PIX, PIX), 1)
    total = jnp.zeros(bias_ref.shape, F32)
    for turn in range(TURNS):
        pick = (turn_index(source, turn) == target).astype(F32)
        total = total + jnp.dot(tacc[turn], pick, preferred_element_type=F32, precision=HIGH)
    bias_ref[...] = total


def gradient_kernel(
    place_ref,
    x_ref, gain_ref, normed_ref, w_ref, dq_ref, own_ref, fl_ref, fr_ref, dout_ref, mixed_ref,
    dx_ref, gain_out_ref, first_ref, second_ref,
):
    dim = x_ref.shape[1]
    n_member, n_tile, depth, half = first_ref.shape
    x32 = x_ref[...].astype(F32)
    inverse = rms(x32)
    d_kv = own_ref[...] + fl_ref[...].astype(F32) + fr_ref[...].astype(F32)
    d_proj = jnp.concatenate([dq_ref[...], d_kv.astype(BF)], axis=1)
    d_out = dout_ref[...]
    d_normed = nt(d_proj, w_ref[...])
    unit = x32 * inverse
    gain_out_ref[...] = jnp.sum(d_normed * unit, axis=0, keepdims=True)
    d_scaled = d_normed * gain_ref[...]
    inner = jnp.mean(d_scaled * x32, axis=-1, keepdims=True)
    dx_ref[...] = (
        d_out.astype(F32) + inverse * d_scaled - x32 * (inverse * inverse * inverse) * inner
    ).astype(BF)
    d_w = tn(normed_ref[...], d_proj)
    d_o = tn(mixed_ref[...], d_out)
    proj_cols = 3 * dim // n_member
    out_cols = dim // n_member
    for m in range(n_member):
        piece = jnp.concatenate(
            [
                d_w[:, m * proj_cols : (m + 1) * proj_cols],
                d_o[:, m * out_cols : (m + 1) * out_cols],
            ],
            axis=1,
        ).astype(BF)
        to_m = place_ref[0] ^ m
        for t in range(n_tile):
            to_t = place_ref[1] ^ t
            part = piece[t * depth : (t + 1) * depth]
            first_ref[to_m, to_t] = part[:, :half]
            second_ref[to_m, to_t] = part[:, half:]


def call(kernel, outs, n_scalar, n_in, scratch=(), name=None):
    return pl.pallas_call(
        kernel,
        out_shape=outs,
        in_specs=[pl.BlockSpec(memory_space=SM)] * n_scalar
        + [pl.BlockSpec(memory_space=VM)] * n_in,
        out_specs=[pl.BlockSpec(memory_space=VM)] * len(outs),
        scratch_shapes=list(scratch),
        name=name,
    )


def shape(dims, kind):
    return jax.ShapeDtypeStruct(dims, kind)


def swapped(value, axis, bit):
    count = lax.axis_size(axis)
    return lax.ppermute(value, axis, [(i, i ^ bit) for i in range(count)])


def passed_along(value, axis, by):
    count = lax.axis_size(axis)
    pairs = [(i, i + by) for i in range(count) if 0 <= i + by < count]
    return lax.ppermute(value, axis, pairs)


def bits_of(count):
    bits = []
    while (1 << len(bits)) < count:
        bits.append(1 << len(bits))
    return bits


def halved(value, dim):
    size = value.shape[dim] // 2
    keep = lax.slice_in_dim(value, 0, size, axis=dim)
    send = lax.slice_in_dim(value, size, 2 * size, axis=dim)
    return keep, send


def shards(states, teacher, w_qkv, w_out, gain, bias, neighbours, valid, orient):
    x = states[0]
    rows, dim = x.shape
    blocks = neighbours.shape[0]
    heads = bias.shape[0]
    n_tile = lax.axis_size("tile")
    n_member = lax.axis_size("member")
    tile = lax.axis_index("tile")
    member = lax.axis_index("member")
    from_left = passed_along(x, "tile", 1)
    from_right = passed_along(x, "tile", -1)
    near_column = jnp.clip(neighbours // ROWS - tile * COL_DEV + 1, 0, 2)
    near = near_column * ROWS + neighbours % ROWS
    pad = ((0, 0), (0, PAD_SLOTS - SLOTS))
    near = jnp.pad(near, pad).reshape(-1)
    turns = jnp.pad(orient, pad).reshape(-1)
    drop = jnp.pad(jnp.where(valid > 0, 0.0, NEG).astype(F32), pad, constant_values=NEG).reshape(-1)
    gain_row = gain.reshape(1, dim)
    bias_rows = bias.reshape(heads * PIX, PIX)

    normed, proj, table = call(
        own_kernel,
        [
            shape((rows, dim), BF),
            shape((rows, 3 * dim), BF),
            shape((TURNS, heads * PIX, 2 * PIX), F32),
        ],
        0, 4, name="own",
    )(x, gain_row, w_qkv, bias_rows)

    out, d_out, mixed, d_q, d_own, d_left, d_right, bias_term = call(
        attention_kernel,
        [
            shape((rows, dim), BF),
            shape((rows, dim), BF),
            shape((rows, dim), BF),
            shape((rows, dim), BF),
            shape((rows, 2 * dim), F32),
            shape((rows, 2 * dim), BF),
            shape((rows, 2 * dim), BF),
            shape((heads * PIX, PIX), F32),
        ],
        3, 9,
        scratch=[
            pltpu.VMEM((3 * rows, 2 * dim), BF),
            pltpu.VMEM((blocks, PAD_SLOTS * PIX, 2 * dim), BF),
            pltpu.VMEM((blocks, heads * PIX, PAD_SLOTS * PIX), F32),
            pltpu.VMEM((rows, dim), BF),
            pltpu.VMEM((3 * rows, 2 * dim), F32),
            pltpu.VMEM((TURNS, heads * PIX, 2 * PIX), F32),
        ],
        name="attention",
    )(near, turns, drop, x, from_left, from_right, proj, table, gain_row, w_qkv, w_out, teacher)

    back_right = passed_along(d_left, "tile", -1)
    back_left = passed_along(d_right, "tile", 1)

    devices = n_tile * n_member
    both = ("tile", "member")
    spread = bias_term.reshape(devices, heads * PIX * PIX // devices)
    mine = jnp.sum(lax.all_to_all(spread, both, 0, 0, tiled=True), axis=0)
    copies = jnp.broadcast_to(mine[None], (devices,) + mine.shape)
    bias_total = lax.all_to_all(copies, both, 0, 0, tiled=True).reshape(bias.shape)

    depth = dim // n_tile
    place = jnp.stack([member, tile]).astype(jnp.int32)
    piece = shape((n_member, n_tile, depth, dim // 2), BF)
    d_x, gain_term, first, second = call(
        gradient_kernel,
        [shape((rows, dim), BF), shape((1, dim), F32), piece, piece],
        1, 10, name="gradient",
    )(place, x, gain_row, normed, w_qkv, d_q, d_own, back_left, back_right, d_out, mixed)

    gain_copies = jnp.broadcast_to(gain_term, (devices, dim))
    gain_total = jnp.sum(lax.all_to_all(gain_copies, both, 0, 0, tiled=True), axis=0)

    tile_bits = [("tile", bit) for bit in bits_of(n_tile)]
    member_bits = [("member", bit) for bit in bits_of(n_member)]
    near_core, across = member_bits[:1], member_bits[1:]
    first_order = near_core + across + tile_bits
    second_order = near_core + tile_bits[:2] + across + tile_bits[2:]
    done = []
    for value, order in ((first, first_order), (second, second_order)):
        left = {"member": [b for a, b in member_bits], "tile": [b for a, b in tile_bits]}
        for k, (axis, bit) in enumerate(order):
            at = left[axis].index(bit)
            value = reduce_bit(value, axis, bit, at, k == len(order) - 1)
            left[axis].pop(at)
        done.append(value.reshape(depth, dim // 2))
    summed = jnp.concatenate(done, axis=1)
    proj_cols = 3 * dim // n_member
    return (
        out[None],
        d_x[None],
        summed[:, :proj_cols],
        summed[:, proj_cols:],
        gain_total,
        bias_total,
    )


def reduce_bit(value, axis, bit, at, last):
    dim = 0 if axis == "member" else 1
    count = value.shape[dim]
    lead, tail = value.shape[:dim], value.shape[dim + 1 :]
    inner = 1 << at
    split = value.reshape(lead + (count // (2 * inner), 2, inner) + tail)
    keep, send = halved(split, dim + 1)
    total = keep.astype(F32) + swapped(send, axis, bit).astype(F32)
    total = total.reshape(lead + (count // 2,) + tail)
    return total if last else total.astype(BF)


def solution(mesh):
    return jax.shard_map(
        shards,
        mesh=mesh,
        in_specs=(
            P("member", "tile", None),
            P("tile", None),
            P(),
            P(),
            P(),
            P(),
            P("tile", None),
            P("tile", None),
            P("tile", None),
        ),
        out_specs=(
            P("member", "tile", None),
            P("member", "tile", None),
            P("tile", "member"),
            P("tile", "member"),
            P(),
            P(),
        ),
        check_vma=False,
    )
```
